32 devices in a mesh: view: 4 (over y, x), space: 8 (over z, core).
Axes of the slice: x: 2, y: 2, z: 4, core: 2. Of those that a mesh axis runs over, the one named last changes fastest.
Arguments:
- views: bfloat16 [4, 1024, 8, 8, 128], P('view', 'space'), may hold values from 0.25 to 4
- tile_dest: int32 [4, 1024], P('view', 'space'), may hold values from 0 to 1023, as said below
- tile_start: int32 [4, 1024], P('view', 'space'), may hold values from 0 to 3
- tile_extent: int32 [4, 1024], P('view', 'space'), may hold values from 4 to 8, as said below
- psf_taps: float32 [4, 2, 31], P('view')
- estimate: float32 [8, 512, 2048], P(None, 'space'), may hold values from 0.5 to 2
Outputs:
- deconvolved: float32 [8, 512, 2048], P(None, 'space')
The draws below stay inside these ranges and needn't reach their ends.
Inputs may be any that keep to these rules, and one draw needn't show every extreme that they name: `tile_dest`: for each view every joined tile id appears exactly once; the 128 tiles of one device of space go to all 8 owner devices (owner = id // 128), exactly 16 to each. tile_start + tile_extent <= 8.
All inputs are finite; a program needn't handle non-finite values.
Results may differ from the reference program's by a relative error of at most 0.0003.
Values may be sent and summed in bfloat16 or wider, within the bound.
A program may use at most 128 MiB of HBM per device.

```python
import math
import jax
import jax.numpy as jnp
from jax import lax

PLANES = 8
ROWS = 64
NX = 2048
TR = 8
TC = 128
RADIUS = 15
TAPS = 31
ITERS = 2
VIEWS = 4
NY = 512
TILES = 128
TOTAL_TILES = 1024
GROUPS = 8
N_SPACE = 8


def route_view(view_key):
    key_offsets, key_order = jax.random.split(view_key)
    offsets = jax.random.permutation(key_offsets, N_SPACE)[:GROUPS].astype(jnp.int32)
    slot_order = jax.random.permutation(key_order, TILES).astype(jnp.int32)
    source_ids = jnp.arange(TOTAL_TILES, dtype=jnp.int32) // TILES
    local_ids = jnp.arange(TOTAL_TILES, dtype=jnp.int32) % TILES
    owners = (source_ids + offsets[local_ids % GROUPS]) % N_SPACE
    return (owners * TILES + slot_order[local_ids]).astype(jnp.int32)


def draw_tile_dest(key, part):
    return jnp.stack([route_view(jax.random.fold_in(key, view)) for view in range(VIEWS)])


def coverage_pair(key):
    key_start, key_extent = jax.random.split(jax.random.fold_in(key, 11))
    start_rows = jax.random.randint(key_start, (VIEWS, TOTAL_TILES), 0, TR // 2)
    spread = jax.random.randint(key_extent, (VIEWS, TOTAL_TILES), 0, 1 << 20)
    extent = TR // 2 + spread % (TR // 2 - start_rows + 1)
    column = jnp.arange(TOTAL_TILES, dtype=jnp.int32)[None, :]
    start_rows = jnp.where(column == 0, 0, jnp.where(column == 1, TR // 2 - 1, start_rows))
    extent = jnp.where(column == 0, TR, jnp.where(column == 1, TR // 2, extent))
    return (start_rows.astype(jnp.int32), extent.astype(jnp.int32))


def draw_tile_start(key, part):
    return coverage_pair(key)[0]


def draw_tile_extent(key, part):
    return coverage_pair(key)[1]


def draw_psf_taps(key, part):
    key_width, key_rough = jax.random.split(jax.random.fold_in(key, 5))
    widths = jnp.exp(jax.random.uniform(key_width, (VIEWS, 2, 1), jnp.float32, jnp.log(6.0), jnp.log(12.0)))
    positions = jnp.arange(TAPS, dtype=jnp.float32)[None, None, :] - RADIUS
    rough = jax.random.uniform(key_rough, (VIEWS, 2, TAPS), jnp.float32, 0.5, 1.5)
    return (jnp.exp(-0.5 * (positions / widths) ** 2) * rough / (2.5066 * widths)).astype(jnp.float32)


def shard_levels(key, shape, cuts, low, largest):
    level, own = 1.0, jax.random.fold_in(key, 6)
    for axis_at, parts in cuts:
        draws = jnp.exp(jax.random.uniform(jax.random.fold_in(own, axis_at), (parts,), jnp.float32, low / len(cuts), largest / len(cuts)))
        level = level * jnp.repeat(draws, shape[axis_at] // parts).reshape([-1 if axis == axis_at else 1 for axis in range(len(shape))])
    return level


def setup_inputs(seed: int = 0) -> dict:
    key_list = jax.random.split(jax.random.key(seed), 7)
    return {
        "views": jnp.clip(jnp.exp(math.log(4.0) - 2.7725887 * jax.random.uniform(key_list[0], (VIEWS, TOTAL_TILES, PLANES, TR, TC), jnp.float32) ** shard_levels(key_list[0], (VIEWS, TOTAL_TILES, PLANES, TR, TC), ((0, 4), (1, 8)), -0.2, 0.2)), 0.25, 4.0).astype(jnp.bfloat16),
        "tile_dest": draw_tile_dest(jax.random.fold_in(key_list[6], 71), 0),
        "tile_start": draw_tile_start(jax.random.fold_in(key_list[6], 71), 0),
        "tile_extent": draw_tile_extent(jax.random.fold_in(key_list[6], 71), 0),
        "psf_taps": draw_psf_taps(jax.random.fold_in(key_list[6], 71), 0),
        "estimate": jnp.clip(jnp.exp(math.log(2.0) - 1.3862944 * jax.random.uniform(key_list[5], (PLANES, NY, NX), jnp.float32) ** shard_levels(key_list[5], (PLANES, NY, NX), ((1, 8),), -0.2, 0.2)), 0.5, 2.0),
    }


def blur_axis(source, kernel, axis, mirrored):
    radius = (kernel.shape[0] - 1) // 2
    widths = [(0, 0), (0, 0), (0, 0)]
    widths[axis] = (radius, radius)
    padded = jnp.pad(source, widths)
    length = source.shape[axis]
    summed = jnp.zeros(source.shape, jnp.float32)
    for offset in range(kernel.shape[0]):
        first_row = offset if mirrored else 2 * radius - offset
        summed = summed + kernel[offset] * lax.slice_in_dim(padded, first_row, first_row + length, axis=axis)
    return summed


def blur_view(source, kernels, mirrored):
    return blur_axis(blur_axis(source, kernels[0], 1, mirrored), kernels[1], 2, mirrored)


def to_strip(tile_data):
    layers = tile_data.shape[1]
    blocks = tile_data.reshape(N_SPACE, ROWS // TR, NX // TC, layers, TR, TC)
    return blocks.transpose(3, 0, 1, 4, 2, 5).reshape(layers, NY, NX)


def register(tile_data, targets, start_rows, extent):
    placed = jnp.zeros_like(tile_data).at[targets].set(tile_data)
    offsets = jnp.arange(TR, dtype=jnp.int32)
    inside = ((offsets[None, :] >= start_rows[:, None]) & (offsets[None, :] < (start_rows + extent)[:, None])).astype(jnp.float32)
    mask_rows = jnp.zeros((TOTAL_TILES, TR), jnp.float32).at[targets].set(inside)
    mask_tiles = jnp.broadcast_to(mask_rows[:, None, :, None], (TOTAL_TILES, 1, TR, TC))
    return to_strip(placed), to_strip(mask_tiles)


def reference(views, tile_dest, tile_start, tile_extent, psf_taps, estimate):
    observed = []
    weights = []
    for view in range(VIEWS):
        image_strip, mask_strip = register(views[view], tile_dest[view], tile_start[view], tile_extent[view])
        observed.append(image_strip)
        weights.append(mask_strip)
    covered = weights[0]
    for view in range(1, VIEWS):
        covered = covered + weights[view]
    divisor = jnp.maximum(covered, 1.0)
    current = estimate
    for iteration in range(ITERS):
        summed = jnp.zeros(current.shape, jnp.float32)
        for view in range(VIEWS):
            blurred = blur_view(current, psf_taps[view], False)
            quotient = weights[view] * observed[view].astype(jnp.float32) / blurred
            summed = summed + blur_view(quotient, psf_taps[view], True)
        current = current * summed / divisor
    return current
```

```python
import functools

import jax
import jax.numpy as jnp
from jax import lax
from jax.experimental import pallas as pl
from jax.experimental.pallas import tpu as pltpu
from jax.sharding import PartitionSpec as P

ITERS = 2
HALO = 16
F32 = jnp.float32
BF16 = jnp.bfloat16


def split_hi_lo(value):
    hi = value.astype(BF16)
    return hi, (value - hi.astype(F32)).astype(BF16)


def banded(taps, index):
    out = jnp.zeros((taps.shape[0],) + index.shape, F32)
    for j in range(taps.shape[1]):
        out = jnp.where(index[None] == j, taps[:, j][:, None, None], out)
    return out


def dot(a, b):
    return jnp.dot(a, b, preferred_element_type=F32)


def update_kernel(ext_ref, wobs_ref, trow_ref, bcol_ref, bmir_ref, tmir_ref, out_ref, s_hi, s_lo, q_s, c_hi, c_lo):
    view_count, plane_count, rows, cols = wobs_ref.shape
    blocks = cols // 256
    ext_rows = ext_ref.shape[1]
    slab = plane_count * rows
    edge = jnp.zeros((view_count, 1, slab, 128), BF16)
    for ref in (s_hi, s_lo):
        ref[:, 0:1] = edge
        ref[:, 2 * blocks + 1 : 2 * blocks + 2] = edge
    q_s[0:1] = edge[0]
    q_s[2 * blocks + 1 : 2 * blocks + 2] = edge[0]
    for p in range(plane_count):
        for b in range(blocks):
            piece = ext_ref[p, :, 256 * b : 256 * b + 256]
            m = dot(trow_ref[...], jnp.concatenate([piece, piece], axis=0))
            hi, lo = split_hi_lo(m)
            for v in range(view_count):
                for h in range(2):
                    part = (slice(v * rows, (v + 1) * rows), slice(128 * h, 128 * h + 128))
                    s_hi[v, 2 * b + h + 1, p * rows : (p + 1) * rows, :] = hi[part]
                    s_lo[v, 2 * b + h + 1, p * rows : (p + 1) * rows, :] = lo[part]

    def windows(load):
        return jnp.concatenate(
            [jnp.concatenate([load(2 * b + i) for i in range(4)], axis=1) for b in range(blocks)], axis=0
        )

    def one_view(v, carry):
        hi = windows(lambda i: s_hi[v, i])
        lo = windows(lambda i: s_lo[v, i])
        blurred = dot(hi, bcol_ref[v, 0]) + dot(hi, bcol_ref[v, 1]) + dot(lo, bcol_ref[v, 0])
        for b in range(blocks):
            for p in range(plane_count):
                first = b * slab + p * rows
                q = wobs_ref[v, p, :, 256 * b : 256 * b + 256].astype(F32) / blurred[first : first + rows]
                q = q.astype(BF16)
                for h in range(2):
                    q_s[2 * b + h + 1, p * rows : (p + 1) * rows, :] = q[:, 128 * h : 128 * h + 128]
        q_all = windows(lambda i: q_s[i])
        c = dot(q_all, bmir_ref[v, 0]) + dot(q_all, bmir_ref[v, 1])
        hi, lo = split_hi_lo(c)
        here = pl.ds(pl.multiple_of(v * rows, rows), rows)
        for b in range(blocks):
            for p in range(plane_count):
                first = b * slab + p * rows
                c_hi[p, here, 256 * b : 256 * b + 256] = hi[first : first + rows]
                c_lo[p, here, 256 * b : 256 * b + 256] = lo[first : first + rows]
        return carry

    lax.fori_loop(0, view_count, one_view, 0)
    for p in range(plane_count):
        for b in range(blocks):
            at = slice(256 * b, 256 * b + 256)
            hi, lo = c_hi[p, :, at], c_lo[p, :, at]
            out_ref[p, :, at] = dot(tmir_ref[...], jnp.concatenate([hi, hi, lo], axis=0))


def update(ext, wobs, trow, bcol, bmir, tmir):
    view_count, plane_count, rows, cols = wobs.shape
    ext_rows = ext.shape[1]
    slab = plane_count * rows
    strips = cols // 128 + 2
    return pl.pallas_call(
        update_kernel,
        out_shape=jax.ShapeDtypeStruct((plane_count, ext_rows, cols), F32),
        in_specs=[pl.BlockSpec(memory_space=pltpu.VMEM)] * 6,
        out_specs=pl.BlockSpec(memory_space=pltpu.VMEM),
        scratch_shapes=[
            pltpu.VMEM((view_count, strips, slab, 128), BF16),
            pltpu.VMEM((view_count, strips, slab, 128), BF16),
            pltpu.VMEM((strips, slab, 128), BF16),
            pltpu.VMEM((plane_count, view_count * rows, cols), BF16),
            pltpu.VMEM((plane_count, view_count * rows, cols), BF16),
        ],
        compiler_params=pltpu.CompilerParams(vmem_limit_bytes=56 * 1024 * 1024),
    )(ext, wobs, trow, bcol, bmir, tmir)


def neighbours(first, last):
    count = lax.axis_size("space")
    up = [(i, i + 1) for i in range(count - 1)]
    down = [(j, i) for i, j in up]
    return lax.ppermute(last, "space", up), lax.ppermute(first, "space", down)


def exchange(tiles, targets, start, extent, view_count, space_count):
    tile_count, planes, tile_rows, tile_cols = tiles.shape
    capacity = tile_count // space_count
    own_planes = planes // view_count
    owners = targets // tile_count
    ids = jnp.arange(tile_count, dtype=jnp.int32)
    earlier = (owners[None, :] == owners[:, None]) & (ids[None, :] < ids[:, None])
    position = owners * capacity + jnp.sum(earlier.astype(jnp.int32), axis=1)
    to_send = (position[None, :] == ids[:, None]).astype(BF16)
    notes = jnp.stack([targets % tile_count, start, extent], axis=1).astype(BF16)
    notes = jnp.broadcast_to(jnp.pad(notes, ((0, 0), (0, 125)))[:, None], (tile_count, view_count, 128))
    payload = jnp.concatenate([tiles.reshape(tile_count, view_count, -1), notes], axis=2)
    outgoing = jnp.einsum("pj,jwx->wpx", to_send, payload, preferred_element_type=F32).astype(BF16)
    incoming = lax.all_to_all(
        outgoing.reshape(view_count * space_count, capacity, -1),
        ("view", "space"),
        split_axis=0,
        concat_axis=0,
        tiled=True,
    ).reshape(view_count, tile_count, -1)
    data = own_planes * tile_rows * tile_cols
    slots = incoming[:, :, data].astype(jnp.int32)
    to_slot = (slots[:, None, :] == ids[None, :, None]).astype(BF16)
    placed = jnp.einsum("vst,vtx->vsx", to_slot, incoming, preferred_element_type=F32)
    first = placed[:, :, data + 1].astype(jnp.int32)
    length = placed[:, :, data + 2].astype(jnp.int32)
    return placed[:, :, :data].astype(BF16), first, length


def body(views, tile_dest, tile_start, tile_extent, psf_taps, estimate):
    view_count, space_count = lax.axis_size("view"), lax.axis_size("space")
    planes, rows, cols = estimate.shape
    tile_count, _, tile_rows, tile_cols = views.shape[1:]
    own = planes // view_count
    down, across = rows // tile_rows, cols // tile_cols
    placed, first, length = exchange(
        views[0], tile_dest[0], tile_start[0], tile_extent[0], view_count, space_count
    )
    observed = placed.reshape(view_count, down, across, own, tile_rows, tile_cols)
    observed = observed.transpose(0, 3, 1, 4, 2, 5)
    offsets = jnp.arange(tile_rows, dtype=jnp.int32)
    inside = (offsets >= first[:, :, None]) & (offsets < (first + length)[:, :, None])
    inside = inside.reshape(view_count, down, across, tile_rows).transpose(0, 1, 3, 2)
    wobs = jnp.where(inside[:, None, :, :, :, None], observed, jnp.zeros((), BF16))
    wobs = wobs.reshape(view_count, own, rows, cols)
    divisor = jnp.maximum(jnp.sum(inside.astype(F32), axis=0), 1.0)
    divisor = jnp.broadcast_to(divisor[..., None], (down, tile_rows, across, tile_cols)).reshape(1, rows, cols)

    taps = lax.all_gather(psf_taps[0], "view", axis=0)
    radius = (taps.shape[2] - 1) // 2
    ext_rows = rows + 2 * HALO
    y = jnp.arange(rows, dtype=jnp.int32)[:, None]
    i = jnp.arange(ext_rows, dtype=jnp.int32)[None, :]
    t_hi, t_lo = split_hi_lo(banded(taps[:, 0], y + HALO + radius - i))
    trow = jnp.concatenate([t_hi, t_lo], axis=2).reshape(view_count * rows, 2 * ext_rows)
    turned = [t.transpose(2, 0, 1).reshape(ext_rows, view_count * rows) for t in (t_hi, t_lo, t_hi)]
    tmir = jnp.concatenate(turned, axis=1)
    k = jnp.arange(512, dtype=jnp.int32)[:, None]
    n = jnp.arange(256, dtype=jnp.int32)[None, :]
    bcol = jnp.stack(split_hi_lo(banded(taps[:, 1], n - k + 128 + radius)), axis=1)
    bmir = jnp.stack(split_hi_lo(banded(taps[:, 1], k - n - 128 + radius)), axis=1)

    current = lax.dynamic_slice_in_dim(estimate, lax.axis_index("view") * own, own, axis=0)
    for iteration in range(ITERS):
        coarse = current.astype(BF16)
        before, after = neighbours(coarse[:, :HALO], coarse[:, rows - HALO :])
        ext = jnp.concatenate([before, coarse, after], axis=1)
        wide = update(ext, wobs, trow, bcol, bmir, tmir)
        before, after = neighbours(wide[:, :HALO], wide[:, HALO + rows :])
        middle = wide[:, HALO : HALO + rows]
        summed = jnp.concatenate(
            [middle[:, :HALO] + before, middle[:, HALO : rows - HALO], middle[:, rows - HALO :] + after], axis=1
        )
        current = current * summed / divisor
    return lax.all_gather(current, "view", axis=0, tiled=True)


def solution(mesh):
    in_specs = (
        P("view", "space", None, None, None),
        P("view", "space"),
        P("view", "space"),
        P("view", "space"),
        P("view", None, None),
        P(None, "space", None),
    )
    out_specs = P(None, "space", None)
    return jax.shard_map(body, mesh=mesh, in_specs=in_specs, out_specs=out_specs, check_vma=False)
```

```python
import functools

import jax
import jax.numpy as jnp
from jax import lax
from jax.experimental import pallas as pl
from jax.experimental.pallas import tpu as pltpu
from jax.sharding import PartitionSpec as P

ITERS = 2
HALO = 16
F32 = jnp.float32
BF16 = jnp.bfloat16


def split_hi_lo(value):
    hi = value.astype(BF16)
    return hi, (value - hi.astype(F32)).astype(BF16)


def banded(taps_ref, v, axis, count, index):
    out = jnp.zeros(index.shape, F32)
    for j in range(count):
        out = jnp.where(index == j, taps_ref[v, axis * count + j], out)
    return split_hi_lo(out)


def bands_kernel(rows, taps_ref, trow_ref, bcol_ref, bmir_ref, tmir_ref):
    view_count, count = taps_ref.shape[0], taps_ref.shape[1] // 2
    radius = (count - 1) // 2
    ext_rows = tmir_ref.shape[0]
    wide = view_count * rows
    y = lax.broadcasted_iota(jnp.int32, (rows, 128), 0)
    i = lax.broadcasted_iota(jnp.int32, (rows, 128), 1)
    o = lax.broadcasted_iota(jnp.int32, (ext_rows, wide), 0)
    lane = lax.broadcasted_iota(jnp.int32, (ext_rows, wide), 1)
    k = lax.broadcasted_iota(jnp.int32, (128, 128), 0)
    n = lax.broadcasted_iota(jnp.int32, (128, 128), 1)
    turned = jnp.zeros((ext_rows, wide), F32)
    for v in range(view_count):
        hi, lo = banded(taps_ref, v, 0, count, y + HALO + radius - i)
        trow_ref[v * rows : (v + 1) * rows, 0:128] = hi
        trow_ref[v * rows : (v + 1) * rows, 128:256] = lo
        index = jnp.where(lane // rows == v, lane - v * rows + HALO + radius - o, -1)
        for j in range(count):
            turned = jnp.where(index == j, taps_ref[v, j], turned)
        for ref, sign in ((bcol_ref, -1), (bmir_ref, 1)):
            for d in range(-1, 4):
                if 0 <= d <= 2:
                    pair = banded(taps_ref, v, 1, count, sign * (k + 128 * d - 128 - n) + radius)
                else:
                    pair = [jnp.zeros((128, 128), BF16)] * 2
                for c in range(2):
                    if 0 <= d + c < 4:
                        for part in range(2):
                            ref[v, part, 128 * (d + c) : 128 * (d + c + 1), 128 * c : 128 * c + 128] = pair[part]
    hi, lo = split_hi_lo(turned)
    for at, part in enumerate((hi, lo, hi)):
        tmir_ref[:, wide * at : wide * (at + 1)] = part


def bands(taps, rows):
    view_count = taps.shape[0]
    return pl.pallas_call(
        functools.partial(bands_kernel, rows),
        out_shape=[
            jax.ShapeDtypeStruct((view_count * rows, 256), BF16),
            jax.ShapeDtypeStruct((view_count, 2, 512, 256), BF16),
            jax.ShapeDtypeStruct((view_count, 2, 512, 256), BF16),
            jax.ShapeDtypeStruct((rows + 2 * HALO, 3 * view_count * rows), BF16),
        ],
        in_specs=[pl.BlockSpec(memory_space=pltpu.SMEM)],
        out_specs=[pl.BlockSpec(memory_space=pltpu.VMEM)] * 4,
    )(taps.reshape(view_count, -1))


def join_kernel(own, me_ref, *refs):
    out_ref, count = refs[-1], len(refs) // 2
    for k in range(count):
        codes, step = refs[2 * k], refs[2 * k + 1]
        first = (me_ref[0] ^ k) * own
        for p in range(own):
            out_ref[first + p] = codes[p].astype(jnp.int32).astype(F32) * step[p]


def gather_views(value, view_count):
    largest = jnp.maximum(jnp.max(jnp.abs(value), axis=1, keepdims=True), 1e-33)
    codes = jnp.round(value * (32767.0 / largest)).astype(jnp.int16)
    step = largest * (1.0 / 32767.0)
    parts = [codes, step]
    for k in range(1, view_count):
        pairs = [(i, i ^ k) for i in range(view_count)]
        parts += [lax.ppermute(codes, "view", pairs), lax.ppermute(step, "view", pairs)]
    own, rows, cols = value.shape
    return pl.pallas_call(
        functools.partial(join_kernel, own),
        out_shape=jax.ShapeDtypeStruct((own * view_count, rows, cols), F32),
        in_specs=[pl.BlockSpec(memory_space=pltpu.SMEM)] + [pl.BlockSpec(memory_space=pltpu.VMEM)] * len(parts),
        out_specs=pl.BlockSpec(memory_space=pltpu.VMEM),
    )(lax.axis_index("view").reshape(1), *parts)


def dot(a, b):
    return jnp.dot(a, b, preferred_element_type=F32)


def update_kernel(ext_ref, wobs_ref, trow_ref, bcol_ref, bmir_ref, tmir_ref, out_ref, s_hi, s_lo, q_s, c_hi, c_lo):
    view_count, plane_count, rows, cols = wobs_ref.shape
    blocks = cols // 256
    ext_rows = ext_ref.shape[1]
    slab = plane_count * rows
    edge = jnp.zeros((view_count, 1, slab, 128), BF16)
    for ref in (s_hi, s_lo):
        ref[:, 0:1] = edge
        ref[:, 2 * blocks + 1 : 2 * blocks + 2] = edge
    q_s[0:1] = edge[0]
    q_s[2 * blocks + 1 : 2 * blocks + 2] = edge[0]
    for p in range(plane_count):
        for b in range(blocks):
            piece = ext_ref[p, :, 256 * b : 256 * b + 256]
            gap = jnp.zeros((128 - ext_rows, 256), BF16)
            m = dot(trow_ref[...], jnp.concatenate([piece, gap, piece, gap], axis=0))
            hi, lo = split_hi_lo(m)
            for v in range(view_count):
                for h in range(2):
                    part = (slice(v * rows, (v + 1) * rows), slice(128 * h, 128 * h + 128))
                    s_hi[v, 2 * b + h + 1, p * rows : (p + 1) * rows, :] = hi[part]
                    s_lo[v, 2 * b + h + 1, p * rows : (p + 1) * rows, :] = lo[part]

    def windows(load):
        return jnp.concatenate(
            [jnp.concatenate([load(2 * b + i) for i in range(4)], axis=1) for b in range(blocks)], axis=0
        )

    def one_view(v, carry):
        hi = windows(lambda i: s_hi[v, i])
        lo = windows(lambda i: s_lo[v, i])
        blurred = dot(hi, bcol_ref[v, 0]) + dot(hi, bcol_ref[v, 1]) + dot(lo, bcol_ref[v, 0])
        for b in range(blocks):
            for p in range(plane_count):
                first = b * slab + p * rows
                q = wobs_ref[v, p, :, 256 * b : 256 * b + 256].astype(F32) / blurred[first : first + rows]
                q = q.astype(BF16)
                for h in range(2):
                    q_s[2 * b + h + 1, p * rows : (p + 1) * rows, :] = q[:, 128 * h : 128 * h + 128]
        q_all = windows(lambda i: q_s[i])
        c = dot(q_all, bmir_ref[v, 0]) + dot(q_all, bmir_ref[v, 1])
        hi, lo = split_hi_lo(c)
        here = pl.ds(pl.multiple_of(v * rows, rows), rows)
        for b in range(blocks):
            for p in range(plane_count):
                first = b * slab + p * rows
                c_hi[p, here, 256 * b : 256 * b + 256] = hi[first : first + rows]
                c_lo[p, here, 256 * b : 256 * b + 256] = lo[first : first + rows]
        return carry

    lax.fori_loop(0, view_count, one_view, 0)
    for p in range(plane_count):
        for b in range(blocks):
            at = slice(256 * b, 256 * b + 256)
            hi, lo = c_hi[p, :, at], c_lo[p, :, at]
            out_ref[p, :, at] = dot(tmir_ref[...], jnp.concatenate([hi, hi, lo], axis=0))


def update(ext, wobs, trow, bcol, bmir, tmir):
    view_count, plane_count, rows, cols = wobs.shape
    ext_rows = ext.shape[1]
    slab = plane_count * rows
    strips = cols // 128 + 2
    return pl.pallas_call(
        update_kernel,
        out_shape=jax.ShapeDtypeStruct((plane_count, ext_rows, cols), F32),
        in_specs=[pl.BlockSpec(memory_space=pltpu.VMEM)] * 6,
        out_specs=pl.BlockSpec(memory_space=pltpu.VMEM),
        scratch_shapes=[
            pltpu.VMEM((view_count, strips, slab, 128), BF16),
            pltpu.VMEM((view_count, strips, slab, 128), BF16),
            pltpu.VMEM((strips, slab, 128), BF16),
            pltpu.VMEM((plane_count, view_count * rows, cols), BF16),
            pltpu.VMEM((plane_count, view_count * rows, cols), BF16),
        ],
        compiler_params=pltpu.CompilerParams(vmem_limit_bytes=56 * 1024 * 1024),
    )(ext, wobs, trow, bcol, bmir, tmir)


def neighbours(first, last):
    count = lax.axis_size("space")
    up = [(i, i + 1) for i in range(count - 1)]
    down = [(j, i) for i, j in up]
    return lax.ppermute(last, "space", up), lax.ppermute(first, "space", down)


def exchange(tiles, targets, start, extent, view_count, space_count):
    tile_count, planes, tile_rows, tile_cols = tiles.shape
    capacity = tile_count // space_count
    own_planes = planes // view_count
    owners = targets // tile_count
    ids = jnp.arange(tile_count, dtype=jnp.int32)
    earlier = (owners[None, :] == owners[:, None]) & (ids[None, :] < ids[:, None])
    position = owners * capacity + jnp.sum(earlier.astype(jnp.int32), axis=1)
    to_send = (position[None, :] == ids[:, None]).astype(BF16)
    notes = jnp.stack([targets % tile_count, start, extent], axis=1).astype(BF16)
    notes = jnp.broadcast_to(jnp.pad(notes, ((0, 0), (0, 125)))[:, None], (tile_count, view_count, 128))
    payload = jnp.concatenate([tiles.reshape(tile_count, view_count, -1), notes], axis=2)
    outgoing = jnp.einsum("pj,jwx->wpx", to_send, payload, preferred_element_type=F32).astype(BF16)
    incoming = lax.all_to_all(
        outgoing.reshape(view_count * space_count, capacity, -1),
        ("view", "space"),
        split_axis=0,
        concat_axis=0,
        tiled=True,
    ).reshape(view_count, tile_count, -1)
    data = own_planes * tile_rows * tile_cols
    slots = incoming[:, :, data].astype(jnp.int32)
    to_slot = (slots[:, None, :] == ids[None, :, None]).astype(BF16)
    placed = jnp.einsum("vst,vtx->vsx", to_slot, incoming, preferred_element_type=F32)
    first = placed[:, :, data + 1].astype(jnp.int32)
    length = placed[:, :, data + 2].astype(jnp.int32)
    return placed[:, :, :data].astype(BF16), first, length


def body(views, tile_dest, tile_start, tile_extent, psf_taps, estimate):
    view_count, space_count = lax.axis_size("view"), lax.axis_size("space")
    planes, rows, cols = estimate.shape
    tile_count, _, tile_rows, tile_cols = views.shape[1:]
    own = planes // view_count
    down, across = rows // tile_rows, cols // tile_cols
    placed, first, length = exchange(
        views[0], tile_dest[0], tile_start[0], tile_extent[0], view_count, space_count
    )
    observed = placed.reshape(view_count, down, across, own, tile_rows, tile_cols)
    observed = observed.transpose(0, 3, 1, 4, 2, 5)
    offsets = jnp.arange(tile_rows, dtype=jnp.int32)
    inside = (offsets >= first[:, :, None]) & (offsets < (first + length)[:, :, None])
    inside = inside.reshape(view_count, down, across, tile_rows).transpose(0, 1, 3, 2)
    wobs = jnp.where(inside[:, None, :, :, :, None], observed, jnp.zeros((), BF16))
    wobs = wobs.reshape(view_count, own, rows, cols)
    divisor = jnp.maximum(jnp.sum(inside.astype(F32), axis=0), 1.0)
    divisor = jnp.broadcast_to(divisor[..., None], (down, tile_rows, across, tile_cols)).reshape(1, rows, cols)

    taps = lax.all_gather(psf_taps[0], "view", axis=0)
    trow, bcol, bmir, tmir = bands(taps, rows)
    current = lax.dynamic_slice_in_dim(estimate, lax.axis_index("view") * own, own, axis=0)
    for iteration in range(ITERS):
        coarse = current.astype(BF16)
        before, after = neighbours(coarse[:, :HALO], coarse[:, rows - HALO :])
        ext = jnp.concatenate([before, coarse, after], axis=1)
        wide = update(ext, wobs, trow, bcol, bmir, tmir)
        before, after = neighbours(wide[:, :HALO], wide[:, HALO + rows :])
        middle = wide[:, HALO : HALO + rows]
        summed = jnp.concatenate(
            [middle[:, :HALO] + before, middle[:, HALO : rows - HALO], middle[:, rows - HALO :] + after], axis=1
        )
        current = current * summed / divisor
    return gather_views(current, view_count)


def solution(mesh):
    in_specs = (
        P("view", "space", None, None, None),
        P("view", "space"),
        P("view", "space"),
        P("view", "space"),
        P("view", None, None),
        P(None, "space", None),
    )
    out_specs = P(None, "space", None)
    return jax.shard_map(body, mesh=mesh, in_specs=in_specs, out_specs=out_specs, check_vma=False)
```

```python
import functools

import jax
import jax.numpy as jnp
from jax import lax
from jax.experimental import pallas as pl
from jax.experimental.pallas import tpu as pltpu
from jax.sharding import PartitionSpec as P

ITERS = 2
HALO = 16
F32 = jnp.float32
BF16 = jnp.bfloat16


def split_hi_lo(value):
    hi = value.astype(BF16)
    return hi, (value - hi.astype(F32)).astype(BF16)


def banded(taps_ref, v, axis, count, index):
    out = jnp.zeros(index.shape, F32)
    for j in range(count):
        out = jnp.where(index == j, taps_ref[v, axis * count + j], out)
    return split_hi_lo(out)


def bands_kernel(rows, taps_ref, trow_ref, bcol_ref, bmir_ref, tmir_ref):
    view_count, count = taps_ref.shape[0], taps_ref.shape[1] // 2
    radius = (count - 1) // 2
    ext_rows = tmir_ref.shape[0]
    wide = view_count * rows
    y = lax.broadcasted_iota(jnp.int32, (rows, 128), 0)
    i = lax.broadcasted_iota(jnp.int32, (rows, 128), 1)
    o = lax.broadcasted_iota(jnp.int32, (ext_rows, wide), 0)
    lane = lax.broadcasted_iota(jnp.int32, (ext_rows, wide), 1)
    k = lax.broadcasted_iota(jnp.int32, (128, 128), 0)
    n = lax.broadcasted_iota(jnp.int32, (128, 128), 1)
    turned = jnp.zeros((ext_rows, wide), F32)
    for v in range(view_count):
        hi, lo = banded(taps_ref, v, 0, count, y + HALO + radius - i)
        trow_ref[v * rows : (v + 1) * rows, 0:128] = hi
        trow_ref[v * rows : (v + 1) * rows, 128:256] = lo
        index = jnp.where(lane // rows == v, lane - v * rows + HALO + radius - o, -1)
        for j in range(count):
            turned = jnp.where(index == j, taps_ref[v, j], turned)
        for ref, sign in ((bcol_ref, -1), (bmir_ref, 1)):
            for d in range(-1, 4):
                if 0 <= d <= 2:
                    pair = banded(taps_ref, v, 1, count, sign * (k + 128 * d - 128 - n) + radius)
                else:
                    pair = [jnp.zeros((128, 128), BF16)] * 2
                for c in range(2):
                    if 0 <= d + c < 4:
                        for part in range(2):
                            ref[v, part, 128 * (d + c) : 128 * (d + c + 1), 128 * c : 128 * c + 128] = pair[part]
    hi, lo = split_hi_lo(turned)
    for at, part in enumerate((hi, lo, hi)):
        tmir_ref[:, wide * at : wide * (at + 1)] = part


def bands(taps, rows):
    view_count = taps.shape[0]
    return pl.pallas_call(
        functools.partial(bands_kernel, rows),
        out_shape=[
            jax.ShapeDtypeStruct((view_count * rows, 256), BF16),
            jax.ShapeDtypeStruct((view_count, 2, 512, 256), BF16),
            jax.ShapeDtypeStruct((view_count, 2, 512, 256), BF16),
            jax.ShapeDtypeStruct((rows + 2 * HALO, 3 * view_count * rows), BF16),
        ],
        in_specs=[pl.BlockSpec(memory_space=pltpu.SMEM)],
        out_specs=[pl.BlockSpec(memory_space=pltpu.VMEM)] * 4,
    )(taps.reshape(view_count, -1))


def join_kernel(own, me_ref, *refs):
    out_ref, count = refs[-1], len(refs) // 4
    rows = out_ref.shape[1]
    for k in range(count):
        inner, inner_step, outer, outer_step = refs[4 * k : 4 * k + 4]
        first = (me_ref[0] ^ k) * own
        for p in range(own):
            out_ref[first + p, HALO : rows - HALO] = inner[p].astype(jnp.int32).astype(F32) * inner_step[p]
            ends = outer[p].astype(jnp.int32).astype(F32) * outer_step[p]
            out_ref[first + p, :HALO] = ends[:HALO]
            out_ref[first + p, rows - HALO :] = ends[HALO:]


def send_views(value, view_count):
    largest = jnp.maximum(jnp.max(jnp.abs(value), axis=1, keepdims=True), 1e-33)
    codes = jnp.round(value * (32767.0 / largest)).astype(jnp.int16)
    step = largest * (1.0 / 32767.0)
    parts = [(codes, step)]
    for k in range(1, view_count):
        pairs = [(i, i ^ k) for i in range(view_count)]
        parts.append((lax.ppermute(codes, "view", pairs), lax.ppermute(step, "view", pairs)))
    return parts


def join_views(inner, outer, own, rows, cols):
    parts = [array for pair in zip(inner, outer) for part in pair for array in part]
    return pl.pallas_call(
        functools.partial(join_kernel, own),
        out_shape=jax.ShapeDtypeStruct((own * len(inner), rows, cols), F32),
        in_specs=[pl.BlockSpec(memory_space=pltpu.SMEM)] + [pl.BlockSpec(memory_space=pltpu.VMEM)] * len(parts),
        out_specs=pl.BlockSpec(memory_space=pltpu.VMEM),
    )(lax.axis_index("view").reshape(1), *parts)


def dot(a, b):
    return jnp.dot(a, b, preferred_element_type=F32)


def windows(load, blocks):
    return jnp.concatenate(
        [jnp.concatenate([load(2 * b + i) for i in range(4)], axis=1) for b in range(blocks)], axis=0
    )


def clear_edges(ref, blocks):
    edge = jnp.zeros((1,) + ref.shape[1:], ref.dtype)
    ref[0:1] = edge
    ref[2 * blocks + 1 : 2 * blocks + 2] = edge


def blur_down(ext_ref, trow_ref, s_hi, s_lo, view_count, rows):
    plane_count, ext_rows, cols = ext_ref.shape
    for v in range(view_count):
        clear_edges(s_hi.at[v], cols // 256)
        clear_edges(s_lo.at[v], cols // 256)
    for p in range(plane_count):
        for b in range(cols // 256):
            piece = ext_ref[p, :, 256 * b : 256 * b + 256]
            gap = jnp.zeros((128 - ext_rows, 256), BF16)
            m = dot(trow_ref[...], jnp.concatenate([piece, gap, piece, gap], axis=0))
            hi, lo = split_hi_lo(m)
            for v in range(view_count):
                for h in range(2):
                    part = (slice(v * rows, (v + 1) * rows), slice(128 * h, 128 * h + 128))
                    s_hi[v, 2 * b + h + 1, p * rows : (p + 1) * rows, :] = hi[part]
                    s_lo[v, 2 * b + h + 1, p * rows : (p + 1) * rows, :] = lo[part]


def blur_across(v, bcol_ref, s_hi, s_lo, blocks):
    hi = windows(lambda i: s_hi[v, i], blocks)
    lo = windows(lambda i: s_lo[v, i], blocks)
    return dot(hi, bcol_ref[v, 0]) + dot(hi, bcol_ref[v, 1]) + dot(lo, bcol_ref[v, 0])


def mirror_across(v, blurred, wobs_ref, bmir_ref, q_s, c_hi, c_lo):
    _, plane_count, rows, cols = wobs_ref.shape
    slab, blocks = plane_count * rows, cols // 256
    for b in range(blocks):
        for p in range(plane_count):
            first = b * slab + p * rows
            q = wobs_ref[v, p, :, 256 * b : 256 * b + 256].astype(F32) / blurred[first : first + rows]
            q = q.astype(BF16)
            for h in range(2):
                q_s[2 * b + h + 1, p * rows : (p + 1) * rows, :] = q[:, 128 * h : 128 * h + 128]
    q_all = windows(lambda i: q_s[i], blocks)
    c = dot(q_all, bmir_ref[v, 0]) + dot(q_all, bmir_ref[v, 1])
    hi, lo = split_hi_lo(c)
    here = pl.ds(pl.multiple_of(v * rows, rows), rows)
    for b in range(blocks):
        for p in range(plane_count):
            first = b * slab + p * rows
            c_hi[p, here, 256 * b : 256 * b + 256] = hi[first : first + rows]
            c_lo[p, here, 256 * b : 256 * b + 256] = lo[first : first + rows]


def mirror_down(tmir_ref, c_hi, c_lo, out_ref):
    for p in range(out_ref.shape[0]):
        for b in range(out_ref.shape[2] // 256):
            at = slice(256 * b, 256 * b + 256)
            hi, lo = c_hi[p, :, at], c_lo[p, :, at]
            out_ref[p, :, at] = dot(tmir_ref[...], jnp.concatenate([hi, hi, lo], axis=0))


def loop_views(view_count, step):
    lax.fori_loop(0, view_count, lambda v, carry: (step(v), carry)[1], 0)


def blur_kernel(ext_ref, trow_ref, bcol_ref, out_ref, s_hi, s_lo):
    view_count, blocks = bcol_ref.shape[0], ext_ref.shape[2] // 256
    blur_down(ext_ref, trow_ref, s_hi, s_lo, view_count, trow_ref.shape[0] // view_count)

    def step(v):
        out_ref[v] = blur_across(v, bcol_ref, s_hi, s_lo, blocks)

    loop_views(view_count, step)


def mirror_kernel(blurred_ref, wobs_ref, bmir_ref, tmir_ref, out_ref, q_s, c_hi, c_lo):
    view_count, _, _, cols = wobs_ref.shape
    clear_edges(q_s, cols // 256)
    loop_views(view_count, lambda v: mirror_across(v, blurred_ref[v], wobs_ref, bmir_ref, q_s, c_hi, c_lo))
    mirror_down(tmir_ref, c_hi, c_lo, out_ref)


def update_kernel(ext_ref, trow_ref, bcol_ref, wobs_ref, bmir_ref, tmir_ref, out_ref, s_hi, s_lo, q_s, c_hi, c_lo):
    view_count, _, rows, cols = wobs_ref.shape
    blur_down(ext_ref, trow_ref, s_hi, s_lo, view_count, rows)
    clear_edges(q_s, cols // 256)

    def step(v):
        blurred = blur_across(v, bcol_ref, s_hi, s_lo, cols // 256)
        mirror_across(v, blurred, wobs_ref, bmir_ref, q_s, c_hi, c_lo)

    loop_views(view_count, step)
    mirror_down(tmir_ref, c_hi, c_lo, out_ref)


def run(kernel, out_shape, scratch, *args):
    return pl.pallas_call(
        kernel,
        out_shape=jax.ShapeDtypeStruct(out_shape, F32),
        in_specs=[pl.BlockSpec(memory_space=pltpu.VMEM)] * len(args),
        out_specs=pl.BlockSpec(memory_space=pltpu.VMEM),
        scratch_shapes=[pltpu.VMEM(shape, BF16) for shape in scratch],
        compiler_params=pltpu.CompilerParams(vmem_limit_bytes=56 * 1024 * 1024),
    )(*args)


def neighbours(first, last):
    count = lax.axis_size("space")
    up = [(i, i + 1) for i in range(count - 1)]
    down = [(j, i) for i, j in up]
    return lax.ppermute(last, "space", up), lax.ppermute(first, "space", down)


def exchange(tiles, targets, start, extent, view_count, space_count):
    tile_count, planes, tile_rows, tile_cols = tiles.shape
    capacity = tile_count // space_count
    own_planes = planes // view_count
    owners = targets // tile_count
    ids = jnp.arange(tile_count, dtype=jnp.int32)
    earlier = (owners[None, :] == owners[:, None]) & (ids[None, :] < ids[:, None])
    position = owners * capacity + jnp.sum(earlier.astype(jnp.int32), axis=1)
    to_send = (position[None, :] == ids[:, None]).astype(BF16)
    notes = jnp.stack([targets % tile_count, start, extent], axis=1).astype(BF16)
    notes = jnp.broadcast_to(jnp.pad(notes, ((0, 0), (0, 125)))[:, None], (tile_count, view_count, 128))
    payload = jnp.concatenate([tiles.reshape(tile_count, view_count, -1), notes], axis=2)
    outgoing = jnp.einsum("pj,jwx->wpx", to_send, payload, preferred_element_type=F32).astype(BF16)
    incoming = lax.all_to_all(
        outgoing.reshape(view_count * space_count, capacity, -1),
        ("view", "space"),
        split_axis=0,
        concat_axis=0,
        tiled=True,
    ).reshape(view_count, tile_count, -1)
    data = own_planes * tile_rows * tile_cols
    slots = incoming[:, :, data].astype(jnp.int32)
    to_slot = (slots[:, None, :] == ids[None, :, None]).astype(BF16)
    placed = jnp.einsum("vst,vtx->vsx", to_slot, incoming, preferred_element_type=F32)
    first = placed[:, :, data + 1].astype(jnp.int32)
    length = placed[:, :, data + 2].astype(jnp.int32)
    return placed[:, :, :data].astype(BF16), first, length


def body(views, tile_dest, tile_start, tile_extent, psf_taps, estimate):
    view_count, space_count = lax.axis_size("view"), lax.axis_size("space")
    planes, rows, cols = estimate.shape
    tile_count, _, tile_rows, tile_cols = views.shape[1:]
    own = planes // view_count
    down, across = rows // tile_rows, cols // tile_cols
    placed, first, length = exchange(
        views[0], tile_dest[0], tile_start[0], tile_extent[0], view_count, space_count
    )
    observed = placed.reshape(view_count, down, across, own, tile_rows, tile_cols)
    observed = observed.transpose(0, 3, 1, 4, 2, 5)
    offsets = jnp.arange(tile_rows, dtype=jnp.int32)
    inside = (offsets >= first[:, :, None]) & (offsets < (first + length)[:, :, None])
    inside = inside.reshape(view_count, down, across, tile_rows).transpose(0, 1, 3, 2)
    wobs = jnp.where(inside[:, None, :, :, :, None], observed, jnp.zeros((), BF16))
    wobs = wobs.reshape(view_count, own, rows, cols)
    covered = jnp.sum(inside.astype(F32), axis=0).reshape(rows, across)
    before, after = neighbours(covered[:HALO], covered[rows - HALO :])
    divisor = jnp.maximum(jnp.concatenate([before, covered, after], axis=0), 1.0)
    ext_rows = rows + 2 * HALO
    divisor = jnp.broadcast_to(divisor[:, :, None], (ext_rows, across, tile_cols)).reshape(1, ext_rows, cols)

    taps = lax.all_gather(psf_taps[0], "view", axis=0)
    trow, bcol, bmir, tmir = bands(taps, rows)
    slab, strips = own * rows, cols // 128 + 2
    wide_shape = (own, ext_rows, cols)
    blur_scratch = [(view_count, strips, slab, 128)] * 2
    mirror_scratch = [(strips, slab, 128)] + [(own, view_count * rows, cols)] * 2
    current = lax.dynamic_slice_in_dim(estimate, lax.axis_index("view") * own, own, axis=0)
    before, after = neighbours(current[:, :HALO], current[:, rows - HALO :])
    current = jnp.concatenate([before, current, after], axis=1)
    blurred_shape = (view_count, slab * (cols // 256), 256)
    blurred = run(blur_kernel, blurred_shape, blur_scratch, current.astype(BF16), trow, bcol)
    wide = run(mirror_kernel, wide_shape, mirror_scratch, blurred, wobs, bmir, tmir)
    for iteration in range(1, ITERS):
        before, after = neighbours(wide[:, : 2 * HALO], wide[:, rows:])
        summed = jnp.concatenate(
            [wide[:, : 2 * HALO] + before, wide[:, 2 * HALO : rows], wide[:, rows:] + after], axis=1
        )
        current = current * summed / divisor
        ext = current.astype(BF16)
        wide = run(update_kernel, wide_shape, blur_scratch + mirror_scratch, ext, trow, bcol, wobs, bmir, tmir)
    before, after = neighbours(wide[:, :HALO], wide[:, HALO + rows :])
    mid = slice(2 * HALO, rows)
    low, high = slice(HALO, 2 * HALO), slice(rows, rows + HALO)
    inner = send_views(current[:, mid] * wide[:, mid] / divisor[:, mid], view_count)
    ends = [
        current[:, low] * (wide[:, low] + before) / divisor[:, low],
        current[:, high] * (wide[:, high] + after) / divisor[:, high],
    ]
    outer = send_views(jnp.concatenate(ends, axis=1), view_count)
    return join_views(inner, outer, own, rows, cols)


def solution(mesh):
    in_specs = (
        P("view", "space", None, None, None),
        P("view", "space"),
        P("view", "space"),
        P("view", "space"),
        P("view", None, None),
        P(None, "space", None),
    )
    out_specs = P(None, "space", None)
    return jax.shard_map(body, mesh=mesh, in_specs=in_specs, out_specs=out_specs, check_vma=False)
```

```python
import functools

import jax
import jax.numpy as jnp
from jax import lax
from jax.experimental import pallas as pl
from jax.experimental.pallas import tpu as pltpu
from jax.sharding import PartitionSpec as P

ITERS = 2
HALO = 16
F32 = jnp.float32
BF16 = jnp.bfloat16


def split_hi_lo(value):
    hi = value.astype(BF16)
    return hi, (value - hi.astype(F32)).astype(BF16)


def banded(taps_ref, v, axis, count, index):
    out = jnp.zeros(index.shape, F32)
    for j in range(count):
        out = jnp.where(index == j, taps_ref[v, axis * count + j], out)
    return split_hi_lo(out)


def bands_kernel(rows, taps_ref, trow_ref, bcol_ref, bmir_ref, tmir_ref):
    view_count, count = taps_ref.shape[0], taps_ref.shape[1] // 2
    radius = (count - 1) // 2
    ext_rows = tmir_ref.shape[0]
    wide = view_count * rows
    y = lax.broadcasted_iota(jnp.int32, (rows, 128), 0)
    i = lax.broadcasted_iota(jnp.int32, (rows, 128), 1)
    o = lax.broadcasted_iota(jnp.int32, (ext_rows, wide), 0)
    lane = lax.broadcasted_iota(jnp.int32, (ext_rows, wide), 1)
    k = lax.broadcasted_iota(jnp.int32, (128, 128), 0)
    n = lax.broadcasted_iota(jnp.int32, (128, 128), 1)
    turned = jnp.zeros((ext_rows, wide), F32)
    for v in range(view_count):
        hi, lo = banded(taps_ref, v, 0, count, y + HALO + radius - i)
        trow_ref[v * rows : (v + 1) * rows, 0:128] = hi
        trow_ref[v * rows : (v + 1) * rows, 128:256] = lo
        index = jnp.where(lane // rows == v, lane - v * rows + HALO + radius - o, -1)
        for j in range(count):
            turned = jnp.where(index == j, taps_ref[v, j], turned)
        for ref, sign in ((bcol_ref, -1), (bmir_ref, 1)):
            for d in range(-1, 4):
                if 0 <= d <= 2:
                    pair = banded(taps_ref, v, 1, count, sign * (k + 128 * d - 128 - n) + radius)
                else:
                    pair = [jnp.zeros((128, 128), BF16)] * 2
                for c in range(2):
                    if 0 <= d + c < 4:
                        for part in range(2):
                            ref[v, part, 128 * (d + c) : 128 * (d + c + 1), 128 * c : 128 * c + 128] = pair[part]
    hi, lo = split_hi_lo(turned)
    for at, part in enumerate((hi, lo, hi)):
        tmir_ref[:, wide * at : wide * (at + 1)] = part


def bands(taps, rows):
    view_count = taps.shape[0]
    return pl.pallas_call(
        functools.partial(bands_kernel, rows),
        out_shape=[
            jax.ShapeDtypeStruct((view_count * rows, 256), BF16),
            jax.ShapeDtypeStruct((view_count, 2, 512, 256), BF16),
            jax.ShapeDtypeStruct((view_count, 2, 512, 256), BF16),
            jax.ShapeDtypeStruct((rows + 2 * HALO, 3 * view_count * rows), BF16),
        ],
        in_specs=[pl.BlockSpec(memory_space=pltpu.SMEM)],
        out_specs=[pl.BlockSpec(memory_space=pltpu.VMEM)] * 4,
    )(taps.reshape(view_count, -1))


def join_kernel(own, me_ref, *refs):
    out_ref, count = refs[-1], len(refs) // 2
    for k in range(count):
        codes, step = refs[2 * k], refs[2 * k + 1]
        first = (me_ref[0] ^ k) * own
        for p in range(own):
            out_ref[first + p] = codes[p].astype(jnp.int32).astype(F32) * step[p]


def gather_views(value, view_count):
    largest = jnp.maximum(jnp.max(jnp.abs(value), axis=1, keepdims=True), 1e-33)
    codes = jnp.round(value * (32767.0 / largest)).astype(jnp.int16)
    step = largest * (1.0 / 32767.0)
    parts = [codes, step]
    for k in range(1, view_count):
        pairs = [(i, i ^ k) for i in range(view_count)]
        parts += [lax.ppermute(codes, "view", pairs), lax.ppermute(step, "view", pairs)]
    own, rows, cols = value.shape
    return pl.pallas_call(
        functools.partial(join_kernel, own),
        out_shape=jax.ShapeDtypeStruct((own * view_count, rows, cols), F32),
        in_specs=[pl.BlockSpec(memory_space=pltpu.SMEM)] + [pl.BlockSpec(memory_space=pltpu.VMEM)] * len(parts),
        out_specs=pl.BlockSpec(memory_space=pltpu.VMEM),
    )(lax.axis_index("view").reshape(1), *parts)


def dot(a, b):
    return jnp.dot(a, b, preferred_element_type=F32)


def windows(load, blocks):
    return jnp.concatenate(
        [jnp.concatenate([load(2 * b + i) for i in range(4)], axis=1) for b in range(blocks)], axis=0
    )


def clear_edges(ref, blocks):
    edge = jnp.zeros((1,) + ref.shape[1:], ref.dtype)
    ref[0:1] = edge
    ref[2 * blocks + 1 : 2 * blocks + 2] = edge


def blur_down(ext_ref, trow_ref, s_hi, s_lo, view_count, rows):
    plane_count, ext_rows, cols = ext_ref.shape
    for v in range(view_count):
        clear_edges(s_hi.at[v], cols // 256)
        clear_edges(s_lo.at[v], cols // 256)
    for p in range(plane_count):
        for b in range(cols // 256):
            piece = ext_ref[p, :, 256 * b : 256 * b + 256]
            gap = jnp.zeros((128 - ext_rows, 256), BF16)
            m = dot(trow_ref[...], jnp.concatenate([piece, gap, piece, gap], axis=0))
            hi, lo = split_hi_lo(m)
            for v in range(view_count):
                for h in range(2):
                    part = (slice(v * rows, (v + 1) * rows), slice(128 * h, 128 * h + 128))
                    s_hi[v, 2 * b + h + 1, p * rows : (p + 1) * rows, :] = hi[part]
                    s_lo[v, 2 * b + h + 1, p * rows : (p + 1) * rows, :] = lo[part]


def blur_across(v, bcol_ref, s_hi, s_lo, blocks):
    hi = windows(lambda i: s_hi[v, i], blocks)
    lo = windows(lambda i: s_lo[v, i], blocks)
    return dot(hi, bcol_ref[v, 0]) + dot(hi, bcol_ref[v, 1]) + dot(lo, bcol_ref[v, 0])


def mirror_across(v, blurred, wobs_ref, bmir_ref, q_s, c_hi, c_lo):
    _, plane_count, rows, cols = wobs_ref.shape
    slab, blocks = plane_count * rows, cols // 256
    for b in range(blocks):
        for p in range(plane_count):
            first = b * slab + p * rows
            q = wobs_ref[v, p, :, 256 * b : 256 * b + 256].astype(F32) / blurred[first : first + rows]
            q = q.astype(BF16)
            for h in range(2):
                q_s[2 * b + h + 1, p * rows : (p + 1) * rows, :] = q[:, 128 * h : 128 * h + 128]
    q_all = windows(lambda i: q_s[i], blocks)
    c = dot(q_all, bmir_ref[v, 0]) + dot(q_all, bmir_ref[v, 1])
    hi, lo = split_hi_lo(c)
    here = pl.ds(pl.multiple_of(v * rows, rows), rows)
    for b in range(blocks):
        for p in range(plane_count):
            first = b * slab + p * rows
            c_hi[p, here, 256 * b : 256 * b + 256] = hi[first : first + rows]
            c_lo[p, here, 256 * b : 256 * b + 256] = lo[first : first + rows]


def mirror_down(tmir_ref, c_hi, c_lo, out_ref):
    for p in range(out_ref.shape[0]):
        for b in range(out_ref.shape[2] // 256):
            at = slice(256 * b, 256 * b + 256)
            hi, lo = c_hi[p, :, at], c_lo[p, :, at]
            out_ref[p, :, at] = dot(tmir_ref[...], jnp.concatenate([hi, hi, lo], axis=0))


def loop_views(view_count, step):
    lax.fori_loop(0, view_count, lambda v, carry: (step(v), carry)[1], 0)


def blur_kernel(ext_ref, trow_ref, bcol_ref, out_ref, s_hi, s_lo):
    view_count, blocks = bcol_ref.shape[0], ext_ref.shape[2] // 256
    blur_down(ext_ref, trow_ref, s_hi, s_lo, view_count, trow_ref.shape[0] // view_count)

    def step(v):
        out_ref[v] = blur_across(v, bcol_ref, s_hi, s_lo, blocks)

    loop_views(view_count, step)


def mirror_kernel(blurred_ref, wobs_ref, bmir_ref, tmir_ref, out_ref, q_s, c_hi, c_lo):
    view_count, _, _, cols = wobs_ref.shape
    clear_edges(q_s, cols // 256)
    loop_views(view_count, lambda v: mirror_across(v, blurred_ref[v], wobs_ref, bmir_ref, q_s, c_hi, c_lo))
    mirror_down(tmir_ref, c_hi, c_lo, out_ref)


def update_kernel(ext_ref, trow_ref, bcol_ref, wobs_ref, bmir_ref, tmir_ref, out_ref, s_hi, s_lo, q_s, c_hi, c_lo):
    view_count, _, rows, cols = wobs_ref.shape
    blur_down(ext_ref, trow_ref, s_hi, s_lo, view_count, rows)
    clear_edges(q_s, cols // 256)

    def step(v):
        blurred = blur_across(v, bcol_ref, s_hi, s_lo, cols // 256)
        mirror_across(v, blurred, wobs_ref, bmir_ref, q_s, c_hi, c_lo)

    loop_views(view_count, step)
    mirror_down(tmir_ref, c_hi, c_lo, out_ref)


def run(kernel, out_shape, scratch, *args):
    return pl.pallas_call(
        kernel,
        out_shape=jax.ShapeDtypeStruct(out_shape, F32),
        in_specs=[pl.BlockSpec(memory_space=pltpu.VMEM)] * len(args),
        out_specs=pl.BlockSpec(memory_space=pltpu.VMEM),
        scratch_shapes=[pltpu.VMEM(shape, BF16) for shape in scratch],
        compiler_params=pltpu.CompilerParams(vmem_limit_bytes=56 * 1024 * 1024),
    )(*args)


def neighbours(first, last):
    count = lax.axis_size("space")
    up = [(i, i + 1) for i in range(count - 1)]
    down = [(j, i) for i, j in up]
    first, last = lax.optimization_barrier((first, last))
    return lax.optimization_barrier((lax.ppermute(last, "space", up), lax.ppermute(first, "space", down)))


def exchange(tiles, targets, start, extent, view_count, space_count):
    tile_count, planes, tile_rows, tile_cols = tiles.shape
    capacity = tile_count // space_count
    own_planes = planes // view_count
    owners = targets // tile_count
    ids = jnp.arange(tile_count, dtype=jnp.int32)
    earlier = (owners[None, :] == owners[:, None]) & (ids[None, :] < ids[:, None])
    position = owners * capacity + jnp.sum(earlier.astype(jnp.int32), axis=1)
    to_send = (position[None, :] == ids[:, None]).astype(BF16)
    notes = jnp.stack([targets % tile_count, start, extent], axis=1).astype(BF16)
    notes = jnp.broadcast_to(jnp.pad(notes, ((0, 0), (0, 125)))[:, None], (tile_count, view_count, 128))
    payload = jnp.concatenate([tiles.reshape(tile_count, view_count, -1), notes], axis=2)
    outgoing = jnp.einsum("pj,jwx->wpx", to_send, payload, preferred_element_type=F32).astype(BF16)
    incoming = lax.all_to_all(
        outgoing.reshape(view_count * space_count, capacity, -1),
        ("view", "space"),
        split_axis=0,
        concat_axis=0,
        tiled=True,
    ).reshape(view_count, tile_count, -1)
    data = own_planes * tile_rows * tile_cols
    slots = incoming[:, :, data].astype(jnp.int32)
    to_slot = (slots[:, None, :] == ids[None, :, None]).astype(BF16)
    placed = jnp.einsum("vst,vtx->vsx", to_slot, incoming, preferred_element_type=F32)
    first = placed[:, :, data + 1].astype(jnp.int32)
    length = placed[:, :, data + 2].astype(jnp.int32)
    return placed[:, :, :data].astype(BF16), first, length


def body(views, tile_dest, tile_start, tile_extent, psf_taps, estimate):
    view_count, space_count = lax.axis_size("view"), lax.axis_size("space")
    planes, rows, cols = estimate.shape
    tile_count, _, tile_rows, tile_cols = views.shape[1:]
    own = planes // view_count
    down, across = rows // tile_rows, cols // tile_cols
    placed, first, length = exchange(
        views[0], tile_dest[0], tile_start[0], tile_extent[0], view_count, space_count
    )
    observed = placed.reshape(view_count, down, across, own, tile_rows, tile_cols)
    observed = observed.transpose(0, 3, 1, 4, 2, 5)
    offsets = jnp.arange(tile_rows, dtype=jnp.int32)
    inside = (offsets >= first[:, :, None]) & (offsets < (first + length)[:, :, None])
    inside = inside.reshape(view_count, down, across, tile_rows).transpose(0, 1, 3, 2)
    wobs = jnp.where(inside[:, None, :, :, :, None], observed, jnp.zeros((), BF16))
    wobs = wobs.reshape(view_count, own, rows, cols)
    divisor = jnp.maximum(jnp.sum(inside.astype(F32), axis=0), 1.0)
    divisor = jnp.broadcast_to(divisor[..., None], (down, tile_rows, across, tile_cols)).reshape(1, rows, cols)

    taps = lax.all_gather(psf_taps[0], "view", axis=0)
    trow, bcol, bmir, tmir = bands(taps, rows)
    slab, strips = own * rows, cols // 128 + 2
    wide_shape = (own, rows + 2 * HALO, cols)
    blur_scratch = [(view_count, strips, slab, 128)] * 2
    mirror_scratch = [(strips, slab, 128)] + [(own, view_count * rows, cols)] * 2
    current = lax.dynamic_slice_in_dim(estimate, lax.axis_index("view") * own, own, axis=0)
    for iteration in range(ITERS):
        coarse = current.astype(BF16)
        before, after = neighbours(coarse[:, :HALO], coarse[:, rows - HALO :])
        ext = jnp.concatenate([before, coarse, after], axis=1)
        if iteration == 0:
            blurred_shape = (view_count, slab * (cols // 256), 256)
            blurred = run(blur_kernel, blurred_shape, blur_scratch, ext, trow, bcol)
            wide = run(mirror_kernel, wide_shape, mirror_scratch, blurred, wobs, bmir, tmir)
        else:
            wide = run(update_kernel, wide_shape, blur_scratch + mirror_scratch, ext, trow, bcol, wobs, bmir, tmir)
        before, after = neighbours(wide[:, :HALO], wide[:, HALO + rows :])
        middle = wide[:, HALO : HALO + rows]
        summed = jnp.concatenate(
            [middle[:, :HALO] + before, middle[:, HALO : rows - HALO], middle[:, rows - HALO :] + after], axis=1
        )
        current = current * summed / divisor
    return gather_views(current, view_count)


def solution(mesh):
    in_specs = (
        P("view", "space", None, None, None),
        P("view", "space"),
        P("view", "space"),
        P("view", "space"),
        P("view", None, None),
        P(None, "space", None),
    )
    out_specs = P(None, "space", None)
    return jax.shard_map(body, mesh=mesh, in_specs=in_specs, out_specs=out_specs, check_vma=False)
```
